128 devices in a mesh: depth: 128 (over x, z, y, core).
Axes of the slice: x: 4, y: 4, z: 4, core: 2. Of those that a mesh axis runs over, the one named last changes fastest.
Arguments:
- initial: bfloat16 [2, 256, 1536], replicated, may hold values from -6 to 6
- weights: bfloat16 [256, 1536, 1536], P('depth'), may hold values from -0.15625 to 0.15625
- biases: float32 [256, 1536], P('depth'), may hold values from -3 to 3
- step_sizes: float32 [256], P('depth'), may hold values from 0.02 to 0.2
Outputs:
- states: bfloat16 [256, 2, 256, 1536], P('depth')
The draws below stay inside these ranges and needn't reach their ends.
All inputs are finite; a program needn't handle non-finite values.
Results may differ from the reference program's by a relative error of at most 0.013.
The reference program's roundings to bfloat16 on the way count: a program that leaves them out, or rounds other values in their place, can miss the bound.
Values may be sent and summed in bfloat16 or wider, within the bound.
A program may use at most 64 MiB of HBM per device.

```python
import math
import jax
import jax.numpy as jnp
from jax import lax

D = 1536
ROWS = 256
LAY_DEV = 2
INTERVAL = 8
LAYERS = 256
GROUPS = 16
N_DEPTH = 128


def draw_step_sizes(key, part):
    first_key, second_key = jax.random.split(jax.random.fold_in(key, 7))
    first_draw = jax.random.uniform(first_key, (LAYERS,), jnp.float32)
    second_draw = jax.random.uniform(second_key, (LAYERS,), jnp.float32)
    coarse_rate = jnp.exp(math.log(0.02) + first_draw * math.log(2.5))
    other_rate = jnp.exp(math.log(0.12) + second_draw * math.log(0.2 / 0.12))
    layer_parity = jnp.arange(LAYERS) % 2
    return jnp.where(layer_parity == 0, coarse_rate, other_rate).astype(jnp.float32)


def block_scale(key, shape, shards, smallest, high):
    def one(dim, blocks):
        steps = jax.random.uniform(jax.random.fold_in(jax.random.fold_in(key, 6), dim), (blocks,), jnp.float32, smallest / len(shards), high / len(shards))
        return jnp.repeat(jnp.exp(steps), shape[dim] // blocks).reshape((-1,) + (1,) * (len(shape) - dim - 1))

    gain = one(*shards[0])
    for cut in shards[1:]:
        gain = gain * one(*cut)
    return gain


def noise(rng, shape, deviation, most, shards=(), held_as=jnp.bfloat16):
    factor_of = block_scale(rng, shape, shards, -0.22, 0.18) if shards else 1.0
    result = jax.random.normal(rng, shape, jnp.float32) * deviation * factor_of
    return jnp.minimum(jnp.maximum(result, -most), most).astype(held_as)


def setup_inputs(seed: int = 0) -> dict:
    key_of = jax.random.split(jax.random.key(seed), 5)
    initial = noise(key_of[0], (2, ROWS, D), 1.0, 6.0)
    weights = noise(key_of[1], (LAYERS, D, D), D ** -0.5, 0.15625, ((0, 128),))
    biases = noise(key_of[2], (LAYERS, D), 0.5, 3.0, ((0, 128),), jnp.float32)
    step_sizes = draw_step_sizes(jax.random.fold_in(key_of[4], 71), 0)
    return {"initial": initial, "weights": weights, "biases": biases, "step_sizes": step_sizes}


def advance(entering, weights, biases, step_sizes):
    state = entering.astype(jnp.float32)
    outputs = []
    for layer in range(LAY_DEV):
        pre = jnp.dot(state.astype(jnp.bfloat16), weights[layer], preferred_element_type=jnp.float32) + biases[layer]
        state = state + step_sizes[layer] * jnp.tanh(pre)
        outputs.append(state)
    return jnp.stack(outputs)


def reference(initial, weights, biases, step_sizes):
    row_count = 2 * ROWS
    start_state = initial.reshape(row_count, D)
    weight_blocks = weights.reshape(N_DEPTH, LAY_DEV, D, D)
    bias_blocks = biases.reshape(N_DEPTH, LAY_DEV, D)
    step_blocks = step_sizes.reshape(N_DEPTH, LAY_DEV)
    entries = jnp.broadcast_to(start_state, (N_DEPTH, row_count, D))

    def leave(item):
        return advance(item[0], item[1], item[2], item[3])[-1].astype(jnp.bfloat16)

    for relax_pass in range(2):
        exits = lax.map(leave, (entries, weight_blocks, bias_blocks, step_blocks))
        entries = jnp.concatenate([start_state[None], exits[:-1]], axis=0)
    third_exits = lax.map(leave, (entries, weight_blocks, bias_blocks, step_blocks))
    fresh = jnp.concatenate([start_state[None], third_exits[:-1]], axis=0)
    residuals = fresh.astype(jnp.float32) - entries.astype(jnp.float32)
    grouped_entries = entries.reshape(GROUPS, INTERVAL, row_count, D)
    grouped_weights = weight_blocks[:, 0].reshape(GROUPS, INTERVAL, D, D)
    grouped_biases = bias_blocks[:, 0].reshape(GROUPS, INTERVAL, D)
    grouped_steps = (INTERVAL * LAY_DEV * step_blocks[:, 0]).reshape(GROUPS, INTERVAL)
    grouped_residuals = residuals.reshape(GROUPS, INTERVAL, row_count, D)

    def one_block(item):
        base, correction, weight, bias, coarse_step, residual = item
        anchor = base.astype(jnp.float32)
        moved = anchor + correction.astype(jnp.float32)

        def coarse_map(value):
            pre = jnp.dot(value.astype(jnp.bfloat16), weight, preferred_element_type=jnp.float32) + bias
            return value + coarse_step * jnp.tanh(pre)

        return ((coarse_map(moved) - coarse_map(anchor)) + residual).astype(jnp.bfloat16)

    def link(correction, item):
        base, weight, bias, coarse_step, residual = item
        message = lax.map(one_block, (base, correction, weight, bias, coarse_step, residual))
        return message, message

    zero_group = jnp.zeros((INTERVAL, row_count, D), jnp.bfloat16)
    _, messages = lax.scan(link, zero_group, (grouped_entries[:-1], grouped_weights[:-1], grouped_biases[:-1], grouped_steps[:-1], grouped_residuals[1:]))
    corrections = jnp.concatenate([zero_group[None], messages], axis=0).reshape(N_DEPTH, row_count, D)
    corrected = entries.astype(jnp.float32) + corrections.astype(jnp.float32)

    def finish(item):
        return advance(item[0], item[1], item[2], item[3]).astype(jnp.bfloat16)

    states = lax.map(finish, (corrected, weight_blocks, bias_blocks, step_blocks))
    return states.reshape(LAYERS, 2, ROWS, D)
```

```python
import functools
import jax
import jax.numpy as jnp
from jax import lax
from jax.experimental import pallas as pl
from jax.experimental.pallas import tpu as pltpu
from jax.sharding import PartitionSpec as P

LAY_DEV = 2
INTERVAL = 8
MESH = pl.DeviceIdType.MESH
F32 = jnp.float32
BF16 = jnp.bfloat16

A_ROWS = 128
N_CHUNK = 3
PASS_COLS = 256
CHAIN_ROWS = (64, 64, 32, 16)
FIRST_MSG = (0, 2, 4, 8)
N_MSG = 16


def kernel(rows, width, start_hbm, w_hbm, b_ref, s_ref, out_hbm,
           w, inbuf, inbox, xout, msgout, tbuf, ubuf, xbuf, states,
           w_sem, start_sem, out_sem, x_send, x_recv, r_send, r_recv, m_send, m_recv):
    n_blocks = rows // A_ROWS
    p = lax.axis_index("depth")
    count = lax.axis_size("depth")
    groups = count // INTERVAL
    group = p // INTERVAL
    is_first = p == 0
    has_next = p < count - 1
    sends_msg = (group >= 1) & (group < groups - 1)
    res_direct = (p + 1 >= INTERVAL) & (p + 1 < 2 * INTERVAL)
    res_back = (p + 1 >= 2 * INTERVAL) & has_next
    res_target = jnp.where(res_direct, p + 1, p + 1 - INTERVAL)
    res_slot = jnp.where(res_direct, 0, 1)
    chunk = width // N_CHUNK

    load_start = pltpu.make_async_copy(start_hbm, inbuf.at[0], start_sem)
    load_start.start()
    load_w = [pltpu.make_async_copy(w_hbm.at[l], w.at[l], w_sem.at[l]) for l in range(LAY_DEV)]
    for c in load_w:
        c.start()

    barrier = pltpu.get_barrier_semaphore()
    peers = 0
    for off in (1, -1, INTERVAL, -INTERVAL, INTERVAL - 1, 1 - INTERVAL):
        ok = (p + off >= 0) & (p + off < count)
        peers = peers + jnp.where(ok, 1, 0)

        @pl.when(ok)
        def _():
            pl.semaphore_signal(barrier, inc=1, device_id=(p + off,), device_id_type=MESH)
    pl.semaphore_wait(barrier, peers)

    @pl.when(group == 0)
    def _():
        def zero(i, _):
            r = pl.multiple_of(i * 16, 16)
            inbox[0, pl.ds(r, 16), :] = jnp.zeros((16, width), BF16)
            return 0
        lax.fori_loop(0, rows // 16, zero, 0)

    def x_copy(k, b):
        r = pl.multiple_of(b * A_ROWS, A_ROWS)
        return pltpu.make_async_remote_copy(
            src_ref=xout.at[k, pl.ds(r, A_ROWS)], dst_ref=inbuf.at[k + 1, pl.ds(r, A_ROWS)],
            send_sem=x_send.at[k, b], recv_sem=x_recv.at[k, b],
            device_id=(p + 1,), device_id_type=MESH)

    def res_copy(m, r, size):
        r = pl.multiple_of(r, size)
        return pltpu.make_async_remote_copy(
            src_ref=xout.at[2, pl.ds(r, size)], dst_ref=inbox.at[res_slot, pl.ds(r, size)],
            send_sem=r_send.at[m], recv_sem=r_recv.at[res_slot, m],
            device_id=(res_target,), device_id_type=MESH)

    def res_wait(slot, m, r, size):
        r = pl.multiple_of(r, size)
        pltpu.make_async_remote_copy(
            src_ref=xout.at[2, pl.ds(r, size)], dst_ref=inbox.at[slot, pl.ds(r, size)],
            send_sem=r_send.at[m], recv_sem=r_recv.at[slot, m],
            device_id=(res_target,), device_id_type=MESH).wait_recv()

    def msg_copy(m, r, size, c):
        r = pl.multiple_of(r, size)
        cols = slice(c * chunk, (c + 1) * chunk)
        return pltpu.make_async_remote_copy(
            src_ref=msgout.at[pl.ds(r, size), cols], dst_ref=inbox.at[0, pl.ds(r, size), cols],
            send_sem=m_send.at[m, c], recv_sem=m_recv.at[m, c],
            device_id=(p + INTERVAL,), device_id_type=MESH)

    def messages(b, body):
        for i, size in enumerate(CHAIN_ROWS):
            if i and CHAIN_ROWS[i - 1] == size:
                continue
            same = [j for j in range(len(CHAIN_ROWS)) if CHAIN_ROWS[j] == size]
            per = A_ROWS // size

            @pl.when((b >= same[0]) & (b <= same[-1]))
            def _():
                def one(j, _):
                    body(FIRST_MSG[same[0]] + (b - same[0]) * per + j, b * A_ROWS + j * size, size)
                    return 0
                lax.fori_loop(0, per, one, 0)

    def relax(k, b, first):
        source = jnp.where(is_first, 0, k)
        rb = pl.multiple_of(b * A_ROWS, A_ROWS)
        rs = pl.ds(rb, A_ROWS)

        @pl.when((k > 0) & jnp.logical_not(is_first))
        def _():
            x_copy(k - 1, b).wait_recv()
        x = inbuf[source, rs, :]
        step0 = s_ref[0]
        for c in range(width // PASS_COLS):
            cols = slice(c * PASS_COLS, (c + 1) * PASS_COLS)
            pre = jnp.dot(x, w[0, :, cols], preferred_element_type=F32) + b_ref[0:1, cols]
            t = jnp.tanh(pre)
            tbuf[rs, cols] = t
            u = x[:, cols].astype(F32) + step0 * t
            ubuf[:, cols] = u
            xbuf[:, cols] = u.astype(BF16)

        @pl.when(first)
        def _():
            load_w[1].wait()
        x1 = xbuf[...]
        step1 = s_ref[1]
        for c in range(width // PASS_COLS):
            cols = slice(c * PASS_COLS, (c + 1) * PASS_COLS)
            pre = jnp.dot(x1, w[1, :, cols], preferred_element_type=F32) + b_ref[1:2, cols]
            u = ubuf[:, cols] + step1 * jnp.tanh(pre)
            xout[k, rs, cols] = u.astype(BF16)

        @pl.when((k < 2) & has_next)
        def _():
            x_copy(k, b).start()

        @pl.when((k == 2) & (res_direct | res_back))
        def _():
            def diff(j, _):
                r = pl.ds(pl.multiple_of(rb + j * 16, 16), 16)
                xout[2, r, :] = (xout[2, r, :].astype(F32) - xout[1, r, :].astype(F32)).astype(BF16)
                return 0
            lax.fori_loop(0, A_ROWS // 16, diff, 0)
            messages(b, lambda m, r, size: res_copy(m, r, size).start())

    def chain(b):
        coarse = (INTERVAL * LAY_DEV) * s_ref[0]
        anchor = jnp.where(is_first, 0, 2)

        def one(m, r0, size):
            r = pl.ds(pl.multiple_of(r0, size), size)

            @pl.when(group == 1)
            def _():
                res_wait(0, m, r0, size)

            @pl.when(group > 1)
            def _():
                for c in range(N_CHUNK):
                    msg_copy(m, r0, size, c).wait_recv()

            @pl.when(sends_msg)
            def _():
                res_wait(1, m, r0, size)
            corr = inbox[0, r, :].astype(F32)
            x = (inbuf[anchor, r, :].astype(F32) + corr).astype(BF16)
            for c in range(N_CHUNK):
                cols = slice(c * chunk, (c + 1) * chunk)
                pre = jnp.dot(x, w[0, :, cols], preferred_element_type=F32) + b_ref[0:1, cols]
                t = jnp.tanh(pre)
                d = inbox[0, r, cols].astype(F32) + coarse * (t - tbuf[r, cols])
                msgout[r, cols] = (d + inbox[1, r, cols].astype(F32)).astype(BF16)
                tbuf[r, cols] = t

                @pl.when(sends_msg)
                def _():
                    msg_copy(m, r0, size, c).start()
        messages(b, one)

    def out_copy(l, b):
        r = pl.ds(pl.multiple_of(b * A_ROWS, A_ROWS), A_ROWS)
        return pltpu.make_async_copy(states.at[l, r], out_hbm.at[l, r], out_sem.at[l, b])

    def finish(b):
        anchor = jnp.where(is_first, 0, 2)
        r = pl.ds(pl.multiple_of(b * A_ROWS, A_ROWS), A_ROWS)
        step0 = s_ref[0]
        step1 = s_ref[1]
        for c in range(width // PASS_COLS):
            cols = slice(c * PASS_COLS, (c + 1) * PASS_COLS)
            u = (inbuf[anchor, r, cols].astype(F32) + inbox[0, r, cols].astype(F32)) + step0 * tbuf[r, cols]
            ubuf[:, cols] = u
            states[0, r, cols] = u.astype(BF16)
        out_copy(0, b).start()
        x1 = states[0, r, :]
        for c in range(width // PASS_COLS):
            cols = slice(c * PASS_COLS, (c + 1) * PASS_COLS)
            pre = jnp.dot(x1, w[1, :, cols], preferred_element_type=F32) + b_ref[1:2, cols]
            u = ubuf[:, cols] + step1 * jnp.tanh(pre)
            states[1, r, cols] = u.astype(BF16)
        out_copy(1, b).start()

    load_start.wait()
    load_w[0].wait()
    lag = jnp.where(group <= 2, 1, jnp.where(group <= 5, 2, jnp.where(group <= 8, 3, 4)))

    def wave(step, _):
        def one_pass(k, _):
            b = step - k

            @pl.when((b >= 0) & (b < n_blocks))
            def _():
                relax(k, b, step == 0)
            return 0
        lax.fori_loop(0, 3, one_pass, 0)
        cb = step - 2 - lag

        @pl.when((cb >= 0) & (cb < n_blocks))
        def _():
            @pl.when(group >= 1)
            def _():
                chain(cb)
            finish(cb)
        return 0

    lax.fori_loop(0, n_blocks + 6, wave, 0)

    def drain(b, _):
        for l in range(LAY_DEV):
            out_copy(l, b).wait()

        @pl.when(has_next)
        def _():
            for k in range(2):
                x_copy(k, b).wait_send()

        @pl.when(res_direct | res_back)
        def _():
            messages(b, lambda m, r, size: res_copy(m, r, size).wait_send())

        @pl.when(sends_msg)
        def _():
            def sent(m, r, size):
                for c in range(N_CHUNK):
                    msg_copy(m, r, size, c).wait_send()
            messages(b, sent)
        return 0

    lax.fori_loop(0, n_blocks, drain, 0)


def local(initial, weights, biases, step_sizes):
    width = initial.shape[2]
    rows = initial.shape[0] * initial.shape[1]
    start = initial.reshape(rows, width)
    n_blocks = rows // A_ROWS
    dma = pltpu.SemaphoreType.DMA
    states = pl.pallas_call(
        functools.partial(kernel, rows, width),
        out_shape=jax.ShapeDtypeStruct((LAY_DEV, rows, width), BF16),
        in_specs=[
            pl.BlockSpec(memory_space=pl.ANY),
            pl.BlockSpec(memory_space=pl.ANY),
            pl.BlockSpec(memory_space=pltpu.VMEM),
            pl.BlockSpec(memory_space=pltpu.SMEM),
        ],
        out_specs=pl.BlockSpec(memory_space=pl.ANY),
        scratch_shapes=[
            pltpu.VMEM((LAY_DEV, width, width), BF16),
            pltpu.VMEM((3, rows, width), BF16),
            pltpu.VMEM((2, rows, width), BF16),
            pltpu.VMEM((3, rows, width), BF16),
            pltpu.VMEM((rows, width), BF16),
            pltpu.VMEM((rows, width), F32),
            pltpu.VMEM((A_ROWS, width), F32),
            pltpu.VMEM((A_ROWS, width), BF16),
            pltpu.VMEM((LAY_DEV, rows, width), BF16),
            dma((LAY_DEV,)),
            dma,
            dma((LAY_DEV, n_blocks)),
            dma((2, n_blocks)),
            dma((2, n_blocks)),
            dma((N_MSG,)),
            dma((2, N_MSG)),
            dma((N_MSG, N_CHUNK)),
            dma((N_MSG, N_CHUNK)),
        ],
        compiler_params=pltpu.CompilerParams(
            collective_id=0, has_side_effects=True, vmem_limit_bytes=56 * 1024 * 1024),
    )(start, weights, biases, step_sizes)
    return states.reshape(LAY_DEV, 2, -1, width)


def solution(mesh):
    placed = (P(), P("depth", None, None), P("depth", None), P("depth"))
    return jax.shard_map(
        local, mesh=mesh, in_specs=placed, out_specs=P("depth", None, None, None), check_vma=False
    )
```

```python
import functools
import jax
import jax.numpy as jnp
from jax import lax
from jax.experimental import pallas as pl
from jax.experimental.pallas import tpu as pltpu
from jax.sharding import PartitionSpec as P

LAY_DEV = 2
INTERVAL = 8
MESH = pl.DeviceIdType.MESH
F32 = jnp.float32
BF16 = jnp.bfloat16

A_ROWS = 128
N_CHUNK = 1
PASS_COLS = 256
CHAIN_ROWS = (16, 16, 16, 16)
FIRST_MSG = tuple(sum(A_ROWS // size for size in CHAIN_ROWS[:i]) for i in range(len(CHAIN_ROWS)))
N_MSG = sum(A_ROWS // size for size in CHAIN_ROWS)


def kernel(rows, width, start_hbm, w_hbm, b_ref, s_ref, out_hbm,
           w, inbuf, inbox, xout, msgout, tbuf, ubuf, xbuf, states,
           w_sem, start_sem, out_sem, x_send, x_recv, r_send, r_recv, m_send, m_recv):
    n_blocks = rows // A_ROWS
    p = lax.axis_index("depth")
    count = lax.axis_size("depth")
    groups = count // INTERVAL
    group = p // INTERVAL
    is_first = p == 0
    has_next = p < count - 1
    sends_msg = (group >= 1) & (group < groups - 1)
    res_direct = (p + 1 >= INTERVAL) & (p + 1 < 2 * INTERVAL)
    res_back = (p + 1 >= 2 * INTERVAL) & has_next
    res_target = jnp.where(res_direct, p + 1, p + 1 - INTERVAL)
    res_slot = jnp.where(res_direct, 0, 1)
    chunk = width // N_CHUNK

    load_start = pltpu.make_async_copy(start_hbm, inbuf.at[0], start_sem)
    load_start.start()
    load_w = [pltpu.make_async_copy(w_hbm.at[l], w.at[l], w_sem.at[l]) for l in range(LAY_DEV)]
    load_w[0].start()

    barrier = pltpu.get_barrier_semaphore()
    peers = 0
    for off in (1, -1, INTERVAL, -INTERVAL, INTERVAL - 1, 1 - INTERVAL):
        ok = (p + off >= 0) & (p + off < count)
        peers = peers + jnp.where(ok, 1, 0)

        @pl.when(ok)
        def _():
            pl.semaphore_signal(barrier, inc=1, device_id=(p + off,), device_id_type=MESH)
    pl.semaphore_wait(barrier, peers)

    @pl.when(group == 0)
    def _():
        def zero(i, _):
            r = pl.multiple_of(i * 16, 16)
            inbox[0, pl.ds(r, 16), :] = jnp.zeros((16, width), BF16)
            return 0
        lax.fori_loop(0, rows // 16, zero, 0)

    def x_copy(k, b):
        r = pl.multiple_of(b * A_ROWS, A_ROWS)
        return pltpu.make_async_remote_copy(
            src_ref=xout.at[k, pl.ds(r, A_ROWS)], dst_ref=inbuf.at[k + 1, pl.ds(r, A_ROWS)],
            send_sem=x_send.at[k, b], recv_sem=x_recv.at[k, b],
            device_id=(p + 1,), device_id_type=MESH)

    def res_copy(m, r, size):
        r = pl.multiple_of(r, size)
        return pltpu.make_async_remote_copy(
            src_ref=xout.at[2, pl.ds(r, size)], dst_ref=inbox.at[res_slot, pl.ds(r, size)],
            send_sem=r_send.at[m], recv_sem=r_recv.at[res_slot, m],
            device_id=(res_target,), device_id_type=MESH)

    def res_wait(slot, m, r, size):
        r = pl.multiple_of(r, size)
        pltpu.make_async_remote_copy(
            src_ref=xout.at[2, pl.ds(r, size)], dst_ref=inbox.at[slot, pl.ds(r, size)],
            send_sem=r_send.at[m], recv_sem=r_recv.at[slot, m],
            device_id=(res_target,), device_id_type=MESH).wait_recv()

    def msg_copy(m, r, size, c):
        r = pl.multiple_of(r, size)
        cols = slice(c * chunk, (c + 1) * chunk)
        return pltpu.make_async_remote_copy(
            src_ref=msgout.at[pl.ds(r, size), cols], dst_ref=inbox.at[0, pl.ds(r, size), cols],
            send_sem=m_send.at[m, c], recv_sem=m_recv.at[m, c],
            device_id=(p + INTERVAL,), device_id_type=MESH)

    def messages(b, body):
        for i, size in enumerate(CHAIN_ROWS):
            if i and CHAIN_ROWS[i - 1] == size:
                continue
            same = [j for j in range(len(CHAIN_ROWS)) if CHAIN_ROWS[j] == size]
            per = A_ROWS // size

            @pl.when((b >= same[0]) & (b <= same[-1]))
            def _():
                def one(j, _):
                    body(FIRST_MSG[same[0]] + (b - same[0]) * per + j, b * A_ROWS + j * size, size)
                    return 0
                lax.fori_loop(0, per, one, 0)

    def relax(k, b, first):
        source = jnp.where(is_first, 0, k)
        rb = pl.multiple_of(b * A_ROWS, A_ROWS)
        rs = pl.ds(rb, A_ROWS)

        @pl.when((k > 0) & jnp.logical_not(is_first))
        def _():
            x_copy(k - 1, b).wait_recv()
        x = inbuf[source, rs, :]
        step0 = s_ref[0]
        for c in range(width // PASS_COLS):
            cols = slice(c * PASS_COLS, (c + 1) * PASS_COLS)
            pre = jnp.dot(x, w[0, :, cols], preferred_element_type=F32) + b_ref[0:1, cols]
            t = jnp.tanh(pre)
            tbuf[rs, cols] = t
            u = x[:, cols].astype(F32) + step0 * t
            ubuf[:, cols] = u
            xbuf[:, cols] = u.astype(BF16)

        @pl.when(first)
        def _():
            load_w[1].wait()
        x1 = xbuf[...]
        step1 = s_ref[1]
        for c in range(width // PASS_COLS):
            cols = slice(c * PASS_COLS, (c + 1) * PASS_COLS)
            pre = jnp.dot(x1, w[1, :, cols], preferred_element_type=F32) + b_ref[1:2, cols]
            u = ubuf[:, cols] + step1 * jnp.tanh(pre)
            xout[k, rs, cols] = u.astype(BF16)

        @pl.when((k < 2) & has_next)
        def _():
            x_copy(k, b).start()

        @pl.when((k == 2) & (res_direct | res_back))
        def _():
            def diff(j, _):
                r = pl.ds(pl.multiple_of(rb + j * 16, 16), 16)
                xout[2, r, :] = (xout[2, r, :].astype(F32) - xout[1, r, :].astype(F32)).astype(BF16)
                return 0
            lax.fori_loop(0, A_ROWS // 16, diff, 0)
            messages(b, lambda m, r, size: res_copy(m, r, size).start())

    def chain(b):
        coarse = (INTERVAL * LAY_DEV) * s_ref[0]
        anchor = jnp.where(is_first, 0, 2)

        def one(m, r0, size):
            r = pl.ds(pl.multiple_of(r0, size), size)

            @pl.when(group == 1)
            def _():
                res_wait(0, m, r0, size)

            @pl.when(group > 1)
            def _():
                for c in range(N_CHUNK):
                    msg_copy(m, r0, size, c).wait_recv()

            @pl.when(sends_msg)
            def _():
                res_wait(1, m, r0, size)
            corr = inbox[0, r, :].astype(F32)
            x = (inbuf[anchor, r, :].astype(F32) + corr).astype(BF16)
            for c in range(N_CHUNK):
                cols = slice(c * chunk, (c + 1) * chunk)
                pre = jnp.dot(x, w[0, :, cols], preferred_element_type=F32) + b_ref[0:1, cols]
                t = jnp.tanh(pre)
                d = inbox[0, r, cols].astype(F32) + coarse * (t - tbuf[r, cols])
                msgout[r, cols] = (d + inbox[1, r, cols].astype(F32)).astype(BF16)
                tbuf[r, cols] = t

                @pl.when(sends_msg)
                def _():
                    msg_copy(m, r0, size, c).start()
        messages(b, one)

    def out_copy(l, b):
        r = pl.ds(pl.multiple_of(b * A_ROWS, A_ROWS), A_ROWS)
        return pltpu.make_async_copy(states.at[l, r], out_hbm.at[l, r], out_sem.at[l, b])

    def finish(b):
        anchor = jnp.where(is_first, 0, 2)
        r = pl.ds(pl.multiple_of(b * A_ROWS, A_ROWS), A_ROWS)
        step0 = s_ref[0]
        step1 = s_ref[1]
        for c in range(width // PASS_COLS):
            cols = slice(c * PASS_COLS, (c + 1) * PASS_COLS)
            u = (inbuf[anchor, r, cols].astype(F32) + inbox[0, r, cols].astype(F32)) + step0 * tbuf[r, cols]
            ubuf[:, cols] = u
            states[0, r, cols] = u.astype(BF16)
        out_copy(0, b).start()
        x1 = states[0, r, :]
        for c in range(width // PASS_COLS):
            cols = slice(c * PASS_COLS, (c + 1) * PASS_COLS)
            pre = jnp.dot(x1, w[1, :, cols], preferred_element_type=F32) + b_ref[1:2, cols]
            u = ubuf[:, cols] + step1 * jnp.tanh(pre)
            states[1, r, cols] = u.astype(BF16)
        out_copy(1, b).start()

    load_start.wait()
    load_w[0].wait()
    load_w[1].start()
    late_finish = group < groups // 2
    odd = lax.rem(p, 2)
    lag = jnp.where(group <= 1, 1 - odd, jnp.where(
        group <= 2, 1, jnp.where(group <= 5, 2, jnp.where(group <= 8, 3, 4))))

    def wave(step, _):
        def one_pass(k, _):
            b = step - k

            @pl.when((b >= 0) & (b < n_blocks))
            def _():
                relax(k, b, step == 0)
            return 0
        lax.fori_loop(0, 3, one_pass, 0)
        cb = step - 2 - lag

        @pl.when((cb >= 0) & (cb < n_blocks))
        def _():
            @pl.when(group >= 1)
            def _():
                chain(cb)

            @pl.when(jnp.logical_not(late_finish))
            def _():
                finish(cb)
        return 0

    lax.fori_loop(0, n_blocks + 6, wave, 0)

    @pl.when(late_finish)
    def _():
        def one_finish(b, _):
            finish(b)
            return 0
        lax.fori_loop(0, n_blocks, one_finish, 0)

    def drain(b, _):
        for l in range(LAY_DEV):
            out_copy(l, b).wait()

        @pl.when(has_next)
        def _():
            for k in range(2):
                x_copy(k, b).wait_send()

        @pl.when(res_direct | res_back)
        def _():
            messages(b, lambda m, r, size: res_copy(m, r, size).wait_send())

        @pl.when(sends_msg)
        def _():
            def sent(m, r, size):
                for c in range(N_CHUNK):
                    msg_copy(m, r, size, c).wait_send()
            messages(b, sent)
        return 0

    lax.fori_loop(0, n_blocks, drain, 0)


def local(initial, weights, biases, step_sizes):
    width = initial.shape[2]
    rows = initial.shape[0] * initial.shape[1]
    start = initial.reshape(rows, width)
    n_blocks = rows // A_ROWS
    dma = pltpu.SemaphoreType.DMA
    states = pl.pallas_call(
        functools.partial(kernel, rows, width),
        out_shape=jax.ShapeDtypeStruct((LAY_DEV, rows, width), BF16),
        in_specs=[
            pl.BlockSpec(memory_space=pl.ANY),
            pl.BlockSpec(memory_space=pl.ANY),
            pl.BlockSpec(memory_space=pltpu.VMEM),
            pl.BlockSpec(memory_space=pltpu.SMEM),
        ],
        out_specs=pl.BlockSpec(memory_space=pl.ANY),
        scratch_shapes=[
            pltpu.VMEM((LAY_DEV, width, width), BF16),
            pltpu.VMEM((3, rows, width), BF16),
            pltpu.VMEM((2, rows, width), BF16),
            pltpu.VMEM((3, rows, width), BF16),
            pltpu.VMEM((rows, width), BF16),
            pltpu.VMEM((rows, width), F32),
            pltpu.VMEM((A_ROWS, width), F32),
            pltpu.VMEM((A_ROWS, width), BF16),
            pltpu.VMEM((LAY_DEV, rows, width), BF16),
            dma((LAY_DEV,)),
            dma,
            dma((LAY_DEV, n_blocks)),
            dma((2, n_blocks)),
            dma((2, n_blocks)),
            dma((N_MSG,)),
            dma((2, N_MSG)),
            dma((N_MSG, N_CHUNK)),
            dma((N_MSG, N_CHUNK)),
        ],
        compiler_params=pltpu.CompilerParams(
            collective_id=0, has_side_effects=True, vmem_limit_bytes=56 * 1024 * 1024),
    )(start, weights, biases, step_sizes)
    return states.reshape(LAY_DEV, 2, -1, width)


def solution(mesh):
    placed = (P(), P("depth", None, None), P("depth", None), P("depth"))
    return jax.shard_map(
        local, mesh=mesh, in_specs=placed, out_specs=P("depth", None, None, None), check_vma=False
    )
```

```python
import functools
import jax
import jax.numpy as jnp
from jax import lax
from jax.experimental import pallas as pl
from jax.experimental.pallas import tpu as pltpu
from jax.sharding import PartitionSpec as P

LAY_DEV = 2
INTERVAL = 8
MESH = pl.DeviceIdType.MESH
F32 = jnp.float32
BF16 = jnp.bfloat16

A_ROWS = 128
PASS_COLS = 256
MSG_ROWS = 16
PER_BLOCK = A_ROWS // MSG_ROWS
EARLY_ROWS = (32, 32, 32, 32)
LATE_ROWS = (16, 16, 16, 16)
EARLY_GROUPS = 2


def kernel(rows, width, start_hbm, w_hbm, b_ref, s_ref, out_hbm,
           w, inbuf, inbox, xout, msgout, tbuf, ubuf, xbuf, states,
           w_sem, start_sem, out_sem, x_send, x_recv, r_send, r_recv, m_send, m_recv):
    n_blocks = rows // A_ROWS
    p = lax.axis_index("depth")
    count = lax.axis_size("depth")
    groups = count // INTERVAL
    group = p // INTERVAL
    is_first = p == 0
    has_next = p < count - 1
    sends_msg = (group >= 1) & (group < groups - 1)
    res_direct = (p + 1 >= INTERVAL) & (p + 1 < 2 * INTERVAL)
    res_back = (p + 1 >= 2 * INTERVAL) & has_next
    res_target = jnp.where(res_direct, p + 1, p + 1 - INTERVAL)
    res_slot = jnp.where(res_direct, 0, 1)

    load_start = pltpu.make_async_copy(start_hbm, inbuf.at[0], start_sem)
    load_start.start()
    load_w = [pltpu.make_async_copy(w_hbm.at[l], w.at[l], w_sem.at[l]) for l in range(LAY_DEV)]
    load_w[0].start()

    barrier = pltpu.get_barrier_semaphore()
    peers = 0
    for off in (1, -1, INTERVAL, -INTERVAL, INTERVAL - 1, 1 - INTERVAL):
        ok = (p + off >= 0) & (p + off < count)
        peers = peers + jnp.where(ok, 1, 0)

        @pl.when(ok)
        def _():
            pl.semaphore_signal(barrier, inc=1, device_id=(p + off,), device_id_type=MESH)
    pl.semaphore_wait(barrier, peers)

    @pl.when(group == 0)
    def _():
        def zero(i, _):
            r = pl.multiple_of(i * 16, 16)
            inbox[0, pl.ds(r, 16), :] = jnp.zeros((16, width), BF16)
            return 0
        lax.fori_loop(0, rows // 16, zero, 0)

    def x_copy(k, b):
        r = pl.multiple_of(b * A_ROWS, A_ROWS)
        return pltpu.make_async_remote_copy(
            src_ref=xout.at[k, pl.ds(r, A_ROWS)], dst_ref=inbuf.at[k + 1, pl.ds(r, A_ROWS)],
            send_sem=x_send.at[k, b], recv_sem=x_recv.at[k, b],
            device_id=(p + 1,), device_id_type=MESH)

    def res_copy(m):
        r = pl.ds(pl.multiple_of(m * MSG_ROWS, MSG_ROWS), MSG_ROWS)
        return pltpu.make_async_remote_copy(
            src_ref=xout.at[2, r], dst_ref=inbox.at[res_slot, r],
            send_sem=r_send.at[m], recv_sem=r_recv.at[res_slot, m],
            device_id=(res_target,), device_id_type=MESH)

    def res_wait(slot, m):
        r = pl.ds(pl.multiple_of(m * MSG_ROWS, MSG_ROWS), MSG_ROWS)
        pltpu.make_async_remote_copy(
            src_ref=xout.at[2, r], dst_ref=inbox.at[slot, r],
            send_sem=r_send.at[m], recv_sem=r_recv.at[slot, m],
            device_id=(res_target,), device_id_type=MESH).wait_recv()

    def msg_copy(m):
        r = pl.ds(pl.multiple_of(m * MSG_ROWS, MSG_ROWS), MSG_ROWS)
        return pltpu.make_async_remote_copy(
            src_ref=msgout.at[r], dst_ref=inbox.at[0, r],
            send_sem=m_send.at[m], recv_sem=m_recv.at[m],
            device_id=(p + INTERVAL,), device_id_type=MESH)

    def messages(first, number, body):
        def one(j, _):
            body(first + j)
            return 0
        lax.fori_loop(0, number, one, 0)

    def relax(k, b, first):
        source = jnp.where(is_first, 0, k)
        rb = pl.multiple_of(b * A_ROWS, A_ROWS)
        rs = pl.ds(rb, A_ROWS)

        @pl.when((k > 0) & jnp.logical_not(is_first))
        def _():
            x_copy(k - 1, b).wait_recv()
        x = inbuf[source, rs, :]
        step0 = s_ref[0]
        for c in range(width // PASS_COLS):
            cols = slice(c * PASS_COLS, (c + 1) * PASS_COLS)
            pre = jnp.dot(x, w[0, :, cols], preferred_element_type=F32) + b_ref[0:1, cols]
            t = jnp.tanh(pre)
            tbuf[rs, cols] = t
            u = x[:, cols].astype(F32) + step0 * t
            ubuf[:, cols] = u
            xbuf[:, cols] = u.astype(BF16)

        @pl.when(first)
        def _():
            load_w[1].wait()
        x1 = xbuf[...]
        step1 = s_ref[1]
        for c in range(width // PASS_COLS):
            cols = slice(c * PASS_COLS, (c + 1) * PASS_COLS)
            pre = jnp.dot(x1, w[1, :, cols], preferred_element_type=F32) + b_ref[1:2, cols]
            u = ubuf[:, cols] + step1 * jnp.tanh(pre)
            xout[k, rs, cols] = u.astype(BF16)

        @pl.when((k < 2) & has_next)
        def _():
            x_copy(k, b).start()

        @pl.when((k == 2) & (res_direct | res_back))
        def _():
            def diff(j, _):
                r = pl.ds(pl.multiple_of(rb + j * 16, 16), 16)
                xout[2, r, :] = (xout[2, r, :].astype(F32) - xout[1, r, :].astype(F32)).astype(BF16)
                return 0
            lax.fori_loop(0, A_ROWS // 16, diff, 0)
            messages(b * PER_BLOCK, PER_BLOCK, lambda m: res_copy(m).start())

    def chain(b):
        coarse = (INTERVAL * LAY_DEV) * s_ref[0]
        anchor = jnp.where(is_first, 0, 2)

        def one(r0, size):
            r0 = pl.multiple_of(r0, size)
            r = pl.ds(r0, size)
            number = size // MSG_ROWS
            m = r0 // MSG_ROWS

            @pl.when(group == 1)
            def _():
                messages(m, number, lambda i: res_wait(0, i))

            @pl.when(group > 1)
            def _():
                messages(m, number, lambda i: msg_copy(i).wait_recv())

            @pl.when(sends_msg)
            def _():
                messages(m, number, lambda i: res_wait(1, i))
            corr = inbox[0, r, :].astype(F32)
            x = (inbuf[anchor, r, :].astype(F32) + corr).astype(BF16)
            if size > MSG_ROWS:
                x = jnp.concatenate([x] * (A_ROWS // size), axis=0)
            pre = jnp.dot(x, w[0], preferred_element_type=F32)[:size] + b_ref[0:1, :]
            t = jnp.tanh(pre)
            d = corr + coarse * (t - tbuf[r, :])
            msgout[r, :] = (d + inbox[1, r, :].astype(F32)).astype(BF16)
            tbuf[r, :] = t

            @pl.when(sends_msg)
            def _():
                messages(m, number, lambda i: msg_copy(i).start())

        early = group <= EARLY_GROUPS
        for size in (64, 32, 16):
            chosen = False
            for i in range(rows // A_ROWS):
                if EARLY_ROWS[i] == size:
                    chosen = chosen | (early & (b == i))
                if LATE_ROWS[i] == size:
                    chosen = chosen | (jnp.logical_not(early) & (b == i))
            if chosen is False:
                continue

            @pl.when(chosen)
            def _():
                def each(j, _):
                    one(b * A_ROWS + j * size, size)
                    return 0
                lax.fori_loop(0, A_ROWS // size, each, 0)

    def out_copy(l, b):
        r = pl.ds(pl.multiple_of(b * A_ROWS, A_ROWS), A_ROWS)
        return pltpu.make_async_copy(states.at[l, r], out_hbm.at[l, r], out_sem.at[l, b])

    def finish(b):
        anchor = jnp.where(is_first, 0, 2)
        r = pl.ds(pl.multiple_of(b * A_ROWS, A_ROWS), A_ROWS)
        step0 = s_ref[0]
        step1 = s_ref[1]
        for c in range(width // PASS_COLS):
            cols = slice(c * PASS_COLS, (c + 1) * PASS_COLS)
            u = (inbuf[anchor, r, cols].astype(F32) + inbox[0, r, cols].astype(F32)) + step0 * tbuf[r, cols]
            ubuf[:, cols] = u
            states[0, r, cols] = u.astype(BF16)
        out_copy(0, b).start()
        x1 = states[0, r, :]
        for c in range(width // PASS_COLS):
            cols = slice(c * PASS_COLS, (c + 1) * PASS_COLS)
            pre = jnp.dot(x1, w[1, :, cols], preferred_element_type=F32) + b_ref[1:2, cols]
            u = ubuf[:, cols] + step1 * jnp.tanh(pre)
            states[1, r, cols] = u.astype(BF16)
        out_copy(1, b).start()

    load_start.wait()
    load_w[0].wait()
    load_w[1].start()
    late_finish = group < groups // 2
    odd = lax.rem(p, 2)
    lag = jnp.where(group <= 1, 1 - odd, jnp.where(
        group <= 2, 1, jnp.where(group <= 5, 2, jnp.where(group <= 8, 3, 4))))

    def wave(step, _):
        def one_pass(k, _):
            b = step - k

            @pl.when((b >= 0) & (b < n_blocks))
            def _():
                relax(k, b, step == 0)
            return 0
        lax.fori_loop(0, 3, one_pass, 0)
        cb = step - 2 - lag

        @pl.when((cb >= 0) & (cb < n_blocks))
        def _():
            @pl.when(group >= 1)
            def _():
                chain(cb)

            @pl.when(jnp.logical_not(late_finish))
            def _():
                finish(cb)
        return 0

    lax.fori_loop(0, n_blocks + 6, wave, 0)

    @pl.when(late_finish)
    def _():
        def one_finish(b, _):
            finish(b)
            return 0
        lax.fori_loop(0, n_blocks, one_finish, 0)

    def drain(b, _):
        for l in range(LAY_DEV):
            out_copy(l, b).wait()

        @pl.when(has_next)
        def _():
            for k in range(2):
                x_copy(k, b).wait_send()

        @pl.when(res_direct | res_back)
        def _():
            messages(b * PER_BLOCK, PER_BLOCK, lambda m: res_copy(m).wait_send())

        @pl.when(sends_msg)
        def _():
            messages(b * PER_BLOCK, PER_BLOCK, lambda m: msg_copy(m).wait_send())
        return 0

    lax.fori_loop(0, n_blocks, drain, 0)


def local(initial, weights, biases, step_sizes):
    width = initial.shape[2]
    rows = initial.shape[0] * initial.shape[1]
    start = initial.reshape(rows, width)
    n_blocks = rows // A_ROWS
    n_msg = rows // MSG_ROWS
    dma = pltpu.SemaphoreType.DMA
    states = pl.pallas_call(
        functools.partial(kernel, rows, width),
        out_shape=jax.ShapeDtypeStruct((LAY_DEV, rows, width), BF16),
        in_specs=[
            pl.BlockSpec(memory_space=pl.ANY),
            pl.BlockSpec(memory_space=pl.ANY),
            pl.BlockSpec(memory_space=pltpu.VMEM),
            pl.BlockSpec(memory_space=pltpu.SMEM),
        ],
        out_specs=pl.BlockSpec(memory_space=pl.ANY),
        scratch_shapes=[
            pltpu.VMEM((LAY_DEV, width, width), BF16),
            pltpu.VMEM((3, rows, width), BF16),
            pltpu.VMEM((2, rows, width), BF16),
            pltpu.VMEM((3, rows, width), BF16),
            pltpu.VMEM((rows, width), BF16),
            pltpu.VMEM((rows, width), F32),
            pltpu.VMEM((A_ROWS, width), F32),
            pltpu.VMEM((A_ROWS, width), BF16),
            pltpu.VMEM((LAY_DEV, rows, width), BF16),
            dma((LAY_DEV,)),
            dma,
            dma((LAY_DEV, n_blocks)),
            dma((2, n_blocks)),
            dma((2, n_blocks)),
            dma((n_msg,)),
            dma((2, n_msg)),
            dma((n_msg,)),
            dma((n_msg,)),
        ],
        compiler_params=pltpu.CompilerParams(
            collective_id=0, has_side_effects=True, vmem_limit_bytes=56 * 1024 * 1024),
    )(start, weights, biases, step_sizes)
    return states.reshape(LAY_DEV, 2, -1, width)


def solution(mesh):
    placed = (P(), P("depth", None, None), P("depth", None), P("depth"))
    return jax.shard_map(
        local, mesh=mesh, in_specs=placed, out_specs=P("depth", None, None, None), check_vma=False
    )
```

```python
import functools
import jax
import jax.numpy as jnp
from jax import lax
from jax.experimental import pallas as pl
from jax.experimental.pallas import tpu as pltpu
from jax.sharding import PartitionSpec as P

LAY_DEV = 2
INTERVAL = 8
MESH = pl.DeviceIdType.MESH
F32 = jnp.float32
BF16 = jnp.bfloat16

A_ROWS = 128
PASS_COLS = 256
MSG_ROWS = 16
PER_BLOCK = A_ROWS // MSG_ROWS
EARLY_ROWS = (32, 32, 32, 32)
LATE_ROWS = (16, 16, 16, 16)
EARLY_GROUPS = 2


def kernel(rows, width, start_hbm, w_hbm, b_ref, s_ref, out_hbm,
           w, inbuf, inbox, xout, msgout, tbuf, ubuf, xbuf, states,
           w_sem, start_sem, out_sem, x_send, x_recv, r_send, r_recv, m_send, m_recv):
    n_blocks = rows // A_ROWS
    p = lax.axis_index("depth")
    count = lax.axis_size("depth")
    groups = count // INTERVAL
    group = p // INTERVAL
    is_first = p == 0
    has_next = p < count - 1
    sends_msg = (group >= 1) & (group < groups - 1)
    res_direct = (p + 1 >= INTERVAL) & (p + 1 < 2 * INTERVAL)
    res_back = (p + 1 >= 2 * INTERVAL) & has_next
    res_target = jnp.where(res_direct, p + 1, p + 1 - INTERVAL)
    res_slot = jnp.where(res_direct, 0, 1)

    load_start = pltpu.make_async_copy(start_hbm, inbuf.at[0], start_sem)
    load_start.start()
    load_w = [pltpu.make_async_copy(w_hbm.at[l], w.at[l], w_sem.at[l]) for l in range(LAY_DEV)]
    load_w[0].start()

    barrier = pltpu.get_barrier_semaphore()
    peers = 0
    for off in (1, -1, INTERVAL, -INTERVAL, INTERVAL - 1, 1 - INTERVAL):
        ok = (p + off >= 0) & (p + off < count)
        peers = peers + jnp.where(ok, 1, 0)

        @pl.when(ok)
        def _():
            pl.semaphore_signal(barrier, inc=1, device_id=(p + off,), device_id_type=MESH)
    pl.semaphore_wait(barrier, peers)

    @pl.when(group == 0)
    def _():
        def zero(i, _):
            r = pl.multiple_of(i * 16, 16)
            inbox[0, pl.ds(r, 16), :] = jnp.zeros((16, width), BF16)
            return 0
        lax.fori_loop(0, rows // 16, zero, 0)

    def x_copy(k, b):
        r = pl.multiple_of(b * A_ROWS, A_ROWS)
        return pltpu.make_async_remote_copy(
            src_ref=xout.at[k, pl.ds(r, A_ROWS)], dst_ref=inbuf.at[k + 1, pl.ds(r, A_ROWS)],
            send_sem=x_send.at[k, b], recv_sem=x_recv.at[k, b],
            device_id=(p + 1,), device_id_type=MESH)

    def res_copy(m):
        r = pl.ds(pl.multiple_of(m * MSG_ROWS, MSG_ROWS), MSG_ROWS)
        return pltpu.make_async_remote_copy(
            src_ref=xout.at[2, r], dst_ref=inbox.at[res_slot, r],
            send_sem=r_send.at[m], recv_sem=r_recv.at[res_slot, m],
            device_id=(res_target,), device_id_type=MESH)

    def res_wait(slot, m):
        r = pl.ds(pl.multiple_of(m * MSG_ROWS, MSG_ROWS), MSG_ROWS)
        pltpu.make_async_remote_copy(
            src_ref=xout.at[2, r], dst_ref=inbox.at[slot, r],
            send_sem=r_send.at[m], recv_sem=r_recv.at[slot, m],
            device_id=(res_target,), device_id_type=MESH).wait_recv()

    def msg_copy(m):
        r = pl.ds(pl.multiple_of(m * MSG_ROWS, MSG_ROWS), MSG_ROWS)
        return pltpu.make_async_remote_copy(
            src_ref=msgout.at[r], dst_ref=inbox.at[0, r],
            send_sem=m_send.at[m], recv_sem=m_recv.at[m],
            device_id=(p + INTERVAL,), device_id_type=MESH)

    def messages(first, number, body):
        def one(j, _):
            body(first + j)
            return 0
        lax.fori_loop(0, number, one, 0)

    def relax(k, b, first):
        source = jnp.where(is_first, 0, k)
        rb = pl.multiple_of(b * A_ROWS, A_ROWS)
        rs = pl.ds(rb, A_ROWS)

        @pl.when((k > 0) & jnp.logical_not(is_first))
        def _():
            x_copy(k - 1, b).wait_recv()
        x = inbuf[source, rs, :]
        step0 = s_ref[0]
        for c in range(width // PASS_COLS):
            cols = slice(c * PASS_COLS, (c + 1) * PASS_COLS)
            pre = jnp.dot(x, w[0, :, cols], preferred_element_type=F32) + b_ref[0:1, cols]
            t = jnp.tanh(pre)
            tbuf[rs, cols] = t
            u = x[:, cols].astype(F32) + step0 * t
            ubuf[:, cols] = u
            xbuf[:, cols] = u.astype(BF16)

        @pl.when(first)
        def _():
            load_w[1].wait()
        x1 = xbuf[...]
        step1 = s_ref[1]
        for c in range(width // PASS_COLS):
            cols = slice(c * PASS_COLS, (c + 1) * PASS_COLS)
            pre = jnp.dot(x1, w[1, :, cols], preferred_element_type=F32) + b_ref[1:2, cols]
            u = ubuf[:, cols] + step1 * jnp.tanh(pre)
            xout[k, rs, cols] = u.astype(BF16)

        @pl.when((k < 2) & has_next)
        def _():
            x_copy(k, b).start()

        @pl.when((k == 2) & (res_direct | res_back))
        def _():
            def diff(j, _):
                r = pl.ds(pl.multiple_of(rb + j * 16, 16), 16)
                xout[2, r, :] = (xout[2, r, :].astype(F32) - xout[1, r, :].astype(F32)).astype(BF16)
                return 0
            lax.fori_loop(0, A_ROWS // 16, diff, 0)
            messages(b * PER_BLOCK, PER_BLOCK, lambda m: res_copy(m).start())

    def chain(b):
        coarse = (INTERVAL * LAY_DEV) * s_ref[0]
        anchor = jnp.where(is_first, 0, 2)

        def one(r0, size):
            r0 = pl.multiple_of(r0, size)
            r = pl.ds(r0, size)
            number = size // MSG_ROWS
            m = r0 // MSG_ROWS

            @pl.when(group == 1)
            def _():
                messages(m, number, lambda i: res_wait(0, i))

            @pl.when(group > 1)
            def _():
                messages(m, number, lambda i: msg_copy(i).wait_recv())

            @pl.when(sends_msg)
            def _():
                messages(m, number, lambda i: res_wait(1, i))
            corr = inbox[0, r, :].astype(F32)
            x = (inbuf[anchor, r, :].astype(F32) + corr).astype(BF16)
            if size > MSG_ROWS:
                x = jnp.concatenate([x] * (A_ROWS // size), axis=0)
            pre = jnp.dot(x, w[0], preferred_element_type=F32)[:size] + b_ref[0:1, :]
            t = jnp.tanh(pre)
            d = corr + coarse * (t - tbuf[r, :])
            msgout[r, :] = (d + inbox[1, r, :].astype(F32)).astype(BF16)
            tbuf[r, :] = t

            @pl.when(sends_msg)
            def _():
                messages(m, number, lambda i: msg_copy(i).start())

        early = group <= EARLY_GROUPS
        for size in (64, 32, 16):
            chosen = False
            for i in range(rows // A_ROWS):
                if EARLY_ROWS[i] == size:
                    chosen = chosen | (early & (b == i))
                if LATE_ROWS[i] == size:
                    chosen = chosen | (jnp.logical_not(early) & (b == i))
            if chosen is False:
                continue

            @pl.when(chosen)
            def _():
                def each(j, _):
                    one(b * A_ROWS + j * size, size)
                    return 0
                lax.fori_loop(0, A_ROWS // size, each, 0)

    def out_copy(l, b):
        r = pl.ds(pl.multiple_of(b * A_ROWS, A_ROWS), A_ROWS)
        return pltpu.make_async_copy(states.at[l, r], out_hbm.at[l, r], out_sem.at[l, b])

    def finish(b):
        anchor = jnp.where(is_first, 0, 2)
        r = pl.ds(pl.multiple_of(b * A_ROWS, A_ROWS), A_ROWS)
        step0 = s_ref[0]
        step1 = s_ref[1]
        for c in range(width // PASS_COLS):
            cols = slice(c * PASS_COLS, (c + 1) * PASS_COLS)
            u = (inbuf[anchor, r, cols].astype(F32) + inbox[0, r, cols].astype(F32)) + step0 * tbuf[r, cols]
            ubuf[:, cols] = u
            states[0, r, cols] = u.astype(BF16)
        out_copy(0, b).start()
        x1 = states[0, r, :]
        for c in range(width // PASS_COLS):
            cols = slice(c * PASS_COLS, (c + 1) * PASS_COLS)
            pre = jnp.dot(x1, w[1, :, cols], preferred_element_type=F32) + b_ref[1:2, cols]
            u = ubuf[:, cols] + step1 * jnp.tanh(pre)
            states[1, r, cols] = u.astype(BF16)
        out_copy(1, b).start()

    load_start.wait()
    load_w[0].wait()
    load_w[1].start()
    late_finish = group < groups - 1
    odd = lax.rem(p, 2)
    lag = jnp.where(group <= 1, 1 - odd, jnp.where(
        group <= 2, 1, jnp.where(group <= 5, 2, jnp.where(group <= 8, 3, 4))))

    def wave(step, _):
        def one_pass(k, _):
            b = step - k

            @pl.when((b >= 0) & (b < n_blocks))
            def _():
                relax(k, b, step == 0)
            return 0
        lax.fori_loop(0, 3, one_pass, 0)
        cb = step - 2 - lag

        @pl.when((cb >= 0) & (cb < n_blocks))
        def _():
            @pl.when(group >= 1)
            def _():
                chain(cb)

            @pl.when(jnp.logical_not(late_finish))
            def _():
                finish(cb)
        return 0

    lax.fori_loop(0, n_blocks + 6, wave, 0)

    @pl.when(late_finish)
    def _():
        def one_finish(b, _):
            finish(b)
            return 0
        lax.fori_loop(0, n_blocks, one_finish, 0)

    def drain(b, _):
        for l in range(LAY_DEV):
            out_copy(l, b).wait()

        @pl.when(has_next)
        def _():
            for k in range(2):
                x_copy(k, b).wait_send()

        @pl.when(res_direct | res_back)
        def _():
            messages(b * PER_BLOCK, PER_BLOCK, lambda m: res_copy(m).wait_send())

        @pl.when(sends_msg)
        def _():
            messages(b * PER_BLOCK, PER_BLOCK, lambda m: msg_copy(m).wait_send())
        return 0

    lax.fori_loop(0, n_blocks, drain, 0)


def local(initial, weights, biases, step_sizes):
    width = initial.shape[2]
    rows = initial.shape[0] * initial.shape[1]
    start = initial.reshape(rows, width)
    n_blocks = rows // A_ROWS
    n_msg = rows // MSG_ROWS
    dma = pltpu.SemaphoreType.DMA
    states = pl.pallas_call(
        functools.partial(kernel, rows, width),
        out_shape=jax.ShapeDtypeStruct((LAY_DEV, rows, width), BF16),
        in_specs=[
            pl.BlockSpec(memory_space=pl.ANY),
            pl.BlockSpec(memory_space=pl.ANY),
            pl.BlockSpec(memory_space=pltpu.VMEM),
            pl.BlockSpec(memory_space=pltpu.SMEM),
        ],
        out_specs=pl.BlockSpec(memory_space=pl.ANY),
        scratch_shapes=[
            pltpu.VMEM((LAY_DEV, width, width), BF16),
            pltpu.VMEM((3, rows, width), BF16),
            pltpu.VMEM((2, rows, width), BF16),
            pltpu.VMEM((3, rows, width), BF16),
            pltpu.VMEM((rows, width), BF16),
            pltpu.VMEM((rows, width), F32),
            pltpu.VMEM((A_ROWS, width), F32),
            pltpu.VMEM((A_ROWS, width), BF16),
            pltpu.VMEM((LAY_DEV, rows, width), BF16),
            dma((LAY_DEV,)),
            dma,
            dma((LAY_DEV, n_blocks)),
            dma((2, n_blocks)),
            dma((2, n_blocks)),
            dma((n_msg,)),
            dma((2, n_msg)),
            dma((n_msg,)),
            dma((n_msg,)),
        ],
        compiler_params=pltpu.CompilerParams(
            collective_id=0, has_side_effects=True, vmem_limit_bytes=56 * 1024 * 1024),
    )(start, weights, biases, step_sizes)
    return states.reshape(LAY_DEV, 2, -1, width)


def solution(mesh):
    placed = (P(), P("depth", None, None), P("depth", None), P("depth"))
    return jax.shard_map(
        local, mesh=mesh, in_specs=placed, out_specs=P("depth", None, None, None), check_vma=False
    )
```
